32 devices in a mesh: term: 8 (over y, x, core), topic: 4 (over z).
Axes of the slice: x: 2, y: 2, z: 4, core: 2. Of those that a mesh axis runs over, the one named last changes fastest.
Arguments:
- factor: bfloat16 [65536, 512], P('term', 'topic'), may hold values from 1e-06 to 0.05, as said below
- tile_values: bfloat16 [65536, 128], P('term'), may hold values from 0.049804688 to 1
- tile_docs: int32 [8, 128], P('term'), may hold values from 0 to 127, as said below
- codes: float32 [512, 128], P('topic', 'term'), may hold values from 0.1 to 2
- gram_stat: float32 [512, 512], P('topic', 'term'), may hold values from 0 to 4
- data_stat: float32 [65536, 512], P('term', 'topic'), may hold values from 0 to 0.4
Outputs:
- codes_out: float32 [512, 128], P('topic', 'term')
- gram_new: float32 [512, 512], P('topic', 'term')
- data_new: float32 [65536, 512], P('term', 'topic')
The draws below stay inside these ranges and needn't reach their ends.
Inputs may be any that keep to these rules, and one draw needn't show every extreme that they name: `tile_docs`: each row lists 128 different document numbers. `factor`: positive entries.
All inputs are finite; a program needn't handle non-finite values.
Results may differ from the reference program's by a relative error of at most 0.0003.
Values may be sent and summed in bfloat16 or wider, within the bound.
No kernel may reach another device: no remote copies, remote signals or barrier semaphores. Data moves between devices by JAX's collectives and lax.ppermute only.
A program may use at most 128 MiB of HBM per device.

```python
import math
import jax
import jax.numpy as jnp
from jax import lax

SLAB = 8192
TILE = 128
ITERS = 3
TERMS = 65536
TOPICS = 512
DOCS = 128
SLABS = 8


def draw_tile_docs(key, part):
    slab_keys = jax.random.split(jax.random.fold_in(key, 11), SLABS)
    picked = jax.vmap(lambda slab_key: jax.random.permutation(slab_key, DOCS)[:TILE])(slab_keys)
    return picked.astype(jnp.int32)


def draw_factor(key, part):
    groups = max(TOPICS // 16, 1)
    term_group = jax.random.randint(jax.random.fold_in(key, 21), (TERMS, 1), 0, groups)
    topic_group = jax.random.randint(jax.random.fold_in(key, 22), (1, TOPICS), 0, groups)
    exponent = jnp.clip(jax.random.normal(jax.random.fold_in(key, 23), (TERMS, TOPICS), jnp.float32), -2.5, 2.5)
    magnitude = jnp.where(term_group == topic_group, jnp.float32(0.004), jnp.float32(0.004 / 300.0))
    return (magnitude * jnp.exp(exponent)).astype(jnp.bfloat16)


def levels(own_key, extent, cuts, least, largest):
    def one(dim, shards_of):
        draws = jax.random.uniform(jax.random.fold_in(jax.random.fold_in(own_key, 6), dim), (shards_of,), jnp.float32, least / len(cuts), largest / len(cuts))
        return jnp.repeat(jnp.exp(draws), extent[dim] // shards_of).reshape((-1,) + (1,) * (len(extent) - dim - 1))

    level = one(*cuts[0])
    for cut in cuts[1:]:
        level = level * one(*cut)
    return level


def setup_inputs(seed: int = 0) -> dict:
    arg_keys = jax.random.split(jax.random.key(seed), 7)
    return {
        "factor": draw_factor(jax.random.fold_in(arg_keys[6], 71), 0),
        "tile_values": jnp.clip(jnp.exp(math.log(1.0) - 2.9996462 * jax.random.uniform(arg_keys[1], (TERMS, TILE), jnp.float32) ** levels(arg_keys[1], (TERMS, TILE), ((0, 8),), -0.2, 0.2)), 0.049804688, 1.0).astype(jnp.bfloat16),
        "tile_docs": draw_tile_docs(jax.random.fold_in(arg_keys[6], 71), 0),
        "codes": jnp.clip(jnp.exp(math.log(2.0) - 2.9957323 * jax.random.uniform(arg_keys[3], (TOPICS, DOCS), jnp.float32) ** levels(arg_keys[3], (TOPICS, DOCS), ((0, 4), (1, 8)), -0.2, 0.2)), 0.1, 2.0),
        "gram_stat": jnp.clip(4.0 * jax.random.uniform(arg_keys[4], (TOPICS, TOPICS), jnp.float32) ** levels(arg_keys[4], (TOPICS, TOPICS), ((0, 4), (1, 8)), -0.2, 0.2), 0.0, 4.0),
        "data_stat": jnp.clip(0.4 * jax.random.uniform(arg_keys[5], (TERMS, TOPICS), jnp.float32) ** levels(arg_keys[5], (TERMS, TOPICS), ((0, 8), (1, 4)), -0.2, 0.2), 0.0, 0.4),
    }


EPSILON = 1e-6
DECAY = 0.5


def reference(factor, tile_values, tile_docs, codes, gram_stat, data_stat):
    onehot = (tile_docs[:, :, None] == jnp.arange(DOCS, dtype=jnp.int32)[None, None, :]).astype(jnp.float32)
    tiles = tile_values.reshape(SLABS, SLAB, TILE).astype(jnp.float32)
    batch = jnp.einsum("svt,stb->svb", tiles, onehot).astype(jnp.bfloat16).reshape(SLABS * SLAB, DOCS)
    gram = jnp.dot(factor.T, factor, preferred_element_type=jnp.float32)
    data = jnp.dot(factor.T, batch, preferred_element_type=jnp.float32)
    current = codes
    for update in range(ITERS):
        applied = jnp.dot(gram, current, precision=lax.Precision.HIGHEST, preferred_element_type=jnp.float32)
        current = current * data / (applied + EPSILON)
    outer = jnp.dot(current, current.T, precision=lax.Precision.HIGHEST, preferred_element_type=jnp.float32)
    gram_new = DECAY * gram_stat + outer / DOCS
    widened = batch.astype(jnp.float32)
    data_new = DECAY * data_stat + jnp.dot(widened, current.T, precision=lax.Precision.HIGHEST, preferred_element_type=jnp.float32) / DOCS
    return current, gram_new, data_new
```

```python
import functools
import jax
import jax.numpy as jnp
from jax import lax
from jax.experimental import pallas as pl
from jax.experimental.pallas import tpu as pltpu
from jax.sharding import PartitionSpec as P

ITERS = 3
EPSILON = 1e-06
DECAY = 0.5
ROW_CHUNKS = 8


VMEM = pl.BlockSpec(memory_space=pltpu.VMEM)
ANY = pl.BlockSpec(memory_space=pl.ANY)
SMEM = pl.BlockSpec(memory_space=pltpu.SMEM)


def contract_rows(left, right):
    return lax.dot_general(
        left, right, (((0,), (0,)), ((), ())), preferred_element_type=jnp.float32
    )


def swap(value, axis, offset):
    return lax.ppermute(
        value, axis, [(i, i ^ offset) for i in range(lax.axis_size(axis))]
    )


def gather_term(piece, chips):
    near = [piece] + [swap(piece, "term", 2 * k) for k in range(1, chips)]
    far = [swap(value, "term", 1) for value in near]
    return [value for pair in zip(near, far) for value in pair]


def split(value):
    high = value.astype(jnp.bfloat16)
    return high, (value - high.astype(jnp.float32)).astype(jnp.bfloat16)


def pairs_of(count):
    return [(i, j) for i in range(count) for j in range(i + 1, count)]


def gram_kernel(groups, place, factor, *rest):
    arrived = rest[: groups - 1]
    keep, send, rows, block, sem = rest[groups - 1 :]
    z, core = place[0], place[1]
    share = rows.shape[1]
    copies = [
        pltpu.make_async_copy(
            factor.at[pl.ds(pl.multiple_of(z * share, share), share)], rows.at[z], sem.at[0]
        )
    ]
    for k in range(1, groups):
        copies.append(
            pltpu.make_async_copy(arrived[k - 1], rows.at[z ^ k], sem.at[k])
        )
    for copy in copies:
        copy.start()
    for copy in copies:
        copy.wait()
    chips, _, piece, _ = keep.shape
    for index, (i, j) in enumerate(pairs_of(groups)):
        block[...] = contract_rows(rows[i], rows[j])
        for chip in range(chips):
            own = pl.multiple_of((2 * chip + core) * piece, piece)
            other = pl.multiple_of((2 * chip + 1 - core) * piece, piece)
            keep[chip, index] = block[pl.ds(own, piece), :]
            send[chip, index] = block[pl.ds(other, piece), :]


def gram_blocks(place, factor, arrived, groups, devices):
    share, width = arrived[0].shape
    shape = (devices // 2, groups * (groups - 1) // 2, width // devices, width)
    return pl.pallas_call(
        functools.partial(gram_kernel, groups),
        out_shape=[jax.ShapeDtypeStruct(shape, jnp.float32)] * 2,
        in_specs=[SMEM, ANY] + [ANY] * (groups - 1),
        out_specs=[VMEM, VMEM],
        scratch_shapes=[
            pltpu.VMEM((groups, share, width), jnp.bfloat16),
            pltpu.VMEM((width, width), jnp.float32),
            pltpu.SemaphoreType.DMA((groups,)),
        ],
        name="gram_blocks",
    )(place, factor, *arrived)


def pair_sum_kernel(place, keep, came, *outs):
    chip = place[2]
    for k, out in enumerate(outs):
        out[...] = keep[chip ^ k] + came[chip ^ k]


def pair_sum(place, keep, came):
    chips = keep.shape[0]
    return pl.pallas_call(
        pair_sum_kernel,
        out_shape=[jax.ShapeDtypeStruct(keep.shape[1:], jnp.float32)] * chips,
        in_specs=[SMEM, VMEM, VMEM],
        out_specs=[VMEM] * chips,
        name="pair_sum",
    )(place, keep, came)


def dot3(left, right):
    dot = functools.partial(jnp.dot, preferred_element_type=jnp.float32)
    return dot(left[0], right[0]) + (dot(left[0], right[1]) + dot(left[1], right[0]))


def update_kernel(devices, groups, place, docs, codes, data, diagonal, stat, old, tiles, *rest):
    pieces = rest[:devices]
    codes_out, gram_new, data_new = rest[devices : devices + 3]
    high, low, cur, blocks, tile_buf, old_buf, piece_sem, tile_sem, old_sem, new_sem = rest[
        devices + 3 :
    ]
    z, term = place[0], place[3]
    width, documents = codes.shape[2], codes.shape[1]
    piece = width // devices
    landings = []
    for k in range(devices):
        row = pl.multiple_of((term ^ k) * piece, piece)
        copy = pltpu.make_async_copy(
            pieces[k], blocks.at[:, pl.ds(row, piece), :], piece_sem.at[k]
        )
        copy.start()
        landings.append(copy)
    rows = old.shape[0] // ROW_CHUNKS
    tile_in, old_in = [], []
    for chunk in range(ROW_CHUNKS):
        span = pl.ds(chunk * rows, rows)
        copy = pltpu.make_async_copy(tiles.at[span], tile_buf.at[span], tile_sem.at[chunk])
        copy.start()
        tile_in.append(copy)
        copy = pltpu.make_async_copy(old.at[span], old_buf.at[span], old_sem.at[chunk])
        copy.start()
        old_in.append(copy)
    for copy in landings:
        copy.wait()

    def place_block(i, j, value):
        at = (pl.ds(i * width, width), pl.ds(j * width, width))
        high[at], low[at] = split(value)

    for i in range(groups):
        place_block(i, i, diagonal[i])
        cur[:, pl.ds(i * width, width)] = codes[i]
    for index, (i, j) in enumerate(pairs_of(groups)):
        value = blocks[index]
        place_block(i, j, value)
        place_block(j, i, value.T)

    for _ in range(ITERS):
        applied = dot3(split(cur[...]), (high[...], low[...]))
        for i in range(groups):
            at = pl.ds(i * width, width)
            cur[:, at] = cur[:, at] * data[i] / (applied[:, i * width : (i + 1) * width] + EPSILON)

    own = cur[:, pl.ds(pl.multiple_of(z * width, width), width)]
    own_pair = split(own / documents)
    onehot = (
        docs[...] == lax.broadcasted_iota(jnp.int32, (docs.shape[0], documents), 1)
    ).astype(jnp.bfloat16)
    picked = [
        jnp.dot(onehot, value, preferred_element_type=jnp.float32).astype(jnp.bfloat16)
        for value in own_pair
    ]
    stacked = jnp.concatenate(picked, axis=0)
    stores = []
    for chunk in range(ROW_CHUNKS):
        span = pl.ds(chunk * rows, rows)
        tile_in[chunk].wait()
        old_in[chunk].wait()
        tile = tile_buf[span, :]
        old_buf[span, :] = DECAY * old_buf[span, :] + jnp.dot(
            jnp.concatenate([tile, tile], axis=1), stacked, preferred_element_type=jnp.float32
        )
        copy = pltpu.make_async_copy(old_buf.at[span], data_new.at[span], new_sem.at[chunk])
        copy.start()
        stores.append(copy)

    share = documents // devices
    mine = cur[
        pl.ds(pl.multiple_of(term * share, share), share),
        pl.ds(pl.multiple_of(z * width, width), width),
    ]
    codes_out[...] = mine.T
    columns = stat.shape[1]
    first = term * columns
    group = first // width
    other = split(cur[:, pl.ds(pl.multiple_of(group * width, width), width)])
    left = own_pair
    outer = (
        contract_rows(left[0], other[0])
        + (contract_rows(left[0], other[1]) + contract_rows(left[1], other[0]))
    )
    offset = first - group * width
    part = outer[:, :columns]
    for start in range(columns, width, columns):
        part = jnp.where(offset == start, outer[:, start : start + columns], part)
    gram_new[...] = DECAY * stat[...] + part
    for copy in stores:
        copy.wait()


def update(place, docs, codes, data, diagonal, stat, old, tiles, pieces):
    groups, documents, width = codes.shape
    topics = groups * width
    devices = len(pieces)
    return pl.pallas_call(
        functools.partial(update_kernel, devices, groups),
        out_shape=[
            jax.ShapeDtypeStruct((width, documents // devices), jnp.float32),
            jax.ShapeDtypeStruct(stat.shape, jnp.float32),
            jax.ShapeDtypeStruct(old.shape, jnp.float32),
        ],
        in_specs=[SMEM, VMEM, VMEM, VMEM, VMEM, VMEM, ANY, ANY] + [ANY] * devices,
        out_specs=[VMEM, VMEM, ANY],
        scratch_shapes=[
            pltpu.VMEM((topics, topics), jnp.bfloat16),
            pltpu.VMEM((topics, topics), jnp.bfloat16),
            pltpu.VMEM((documents, topics), jnp.float32),
            pltpu.VMEM((groups * (groups - 1) // 2, width, width), jnp.float32),
            pltpu.VMEM(tiles.shape, tiles.dtype),
            pltpu.VMEM(old.shape, old.dtype),
            pltpu.SemaphoreType.DMA((devices,)),
            pltpu.SemaphoreType.DMA((ROW_CHUNKS,)),
            pltpu.SemaphoreType.DMA((ROW_CHUNKS,)),
            pltpu.SemaphoreType.DMA((ROW_CHUNKS,)),
        ],
        name="update",
    )(place, docs, codes, data, diagonal, stat, old, tiles, *pieces)


def per_device(factor, tile_values, tile_docs, codes, gram_stat, data_stat):
    devices, groups = lax.axis_size("term"), lax.axis_size("topic")
    term, z = lax.axis_index("term"), lax.axis_index("topic")
    chips = devices // 2
    rows, width = factor.shape
    share = rows // groups
    mine = codes.shape[1]
    documents = mine * devices
    piece = width // devices
    place = jnp.stack([z, term % 2, term // 2, term]).astype(jnp.int32)

    order = [k for k in range(2, groups, 2)] + [k for k in range(1, groups, 2)]
    arrived = {}
    for k in order:
        block = lax.dynamic_slice_in_dim(factor, (z ^ k) * share, share, 0)
        arrived[k] = swap(block, "topic", k)

    docs = tile_docs.reshape(-1, 1)
    onehot = (docs == jnp.arange(documents, dtype=jnp.int32)[None, :]).astype(jnp.float32)
    by_tile = contract_rows(tile_values, factor)
    data_part = lax.dot_general(
        onehot, by_tile, (((0,), (0,)), ((), ())),
        precision=lax.Precision.HIGHEST, preferred_element_type=jnp.float32,
    )
    diagonal_part = contract_rows(factor, factor)
    early = jnp.concatenate(
        [data_part.reshape(devices, mine, width), diagonal_part.reshape(devices, piece, width)],
        axis=1,
    )
    early = jnp.sum(lax.all_to_all(early, "term", 0, 0, tiled=True), axis=0)
    early = jnp.concatenate([codes.T, early], axis=0)
    by_group = jnp.stack([early] + [swap(early, "topic", k) for k in range(1, groups)])
    by_group = by_group[z ^ jnp.arange(groups, dtype=jnp.int32)]
    by_term = jnp.stack(gather_term(by_group, chips), axis=1)
    by_term = jnp.take(by_term, term ^ jnp.arange(devices, dtype=jnp.int32), axis=1)
    codes_all = by_term[:, :, :mine].reshape(groups, documents, width)
    data_all = by_term[:, :, mine : 2 * mine].reshape(groups, documents, width)
    diagonal_all = by_term[:, :, 2 * mine :].reshape(groups, width, width)

    keep, send = gram_blocks(
        place, factor, [arrived[k] for k in range(1, groups)], groups, devices
    )
    sums = pair_sum(place, keep, swap(send, "term", 1))
    total = sums[0]
    for part in [swap(sums[k], "term", 2 * k) for k in range(1, chips)]:
        total = total + part
    whole = total
    for part in [swap(total, "topic", k) for k in order]:
        whole = whole + part
    pieces = gather_term(whole, chips)
    return update(
        place, docs, codes_all, data_all, diagonal_all, gram_stat, data_stat, tile_values, pieces
    )


def solution(mesh):
    placed = (
        P("term", "topic"),
        P("term", None),
        P("term", None),
        P("topic", "term"),
        P("topic", "term"),
        P("term", "topic"),
    )
    return jax.shard_map(
        per_device,
        mesh=mesh,
        in_specs=placed,
        out_specs=(P("topic", "term"), P("topic", "term"), P("term", "topic")),
        check_vma=False,
    )
```

```python
import functools
import jax
import jax.numpy as jnp
from jax import lax
from jax.experimental import pallas as pl
from jax.experimental.pallas import tpu as pltpu
from jax.sharding import PartitionSpec as P


ITERS = 3
EPSILON = 1e-06
DECAY = 0.5
ROW_CHUNKS = 8
UPDATE_GRANT = 53 * 2**20


VMEM = pl.BlockSpec(memory_space=pltpu.VMEM)
ANY = pl.BlockSpec(memory_space=pl.ANY)
HBM = pl.BlockSpec(memory_space=pltpu.HBM)
SMEM = pl.BlockSpec(memory_space=pltpu.SMEM)


def contract_rows(left, right):
    return lax.dot_general(
        left, right, (((0,), (0,)), ((), ())), preferred_element_type=jnp.float32
    )


def swap(value, axis, offset):
    return lax.ppermute(
        value, axis, [(i, i ^ offset) for i in range(lax.axis_size(axis))]
    )


def gather_term(piece, chips):
    near = [piece] + [swap(piece, "term", 2 * k) for k in range(1, chips)]
    far = [swap(value, "term", 1) for value in near]
    return [value for pair in zip(near, far) for value in pair]


def split(value):
    high = value.astype(jnp.bfloat16)
    return high, (value - high.astype(jnp.float32)).astype(jnp.bfloat16)


def pairs_of(count):
    return [(i, j) for i in range(count) for j in range(i + 1, count)]


def gram_kernel(groups, place, factor, *rest):
    arrived = rest[: groups - 1]
    out, rows, block, sem = rest[groups - 1 :]
    z = place[0]
    share = rows.shape[1]
    copies = [
        pltpu.make_async_copy(
            factor.at[pl.ds(pl.multiple_of(z * share, share), share)], rows.at[z], sem.at[0]
        )
    ]
    for k in range(1, groups):
        copies.append(pltpu.make_async_copy(arrived[k - 1], rows.at[z ^ k], sem.at[k]))
    for copy in copies:
        copy.start()
    for copy in copies:
        copy.wait()
    devices, _, piece, _ = out.shape
    for index, (i, j) in enumerate(pairs_of(groups)):
        block[...] = contract_rows(rows[i], rows[j])
        for device in range(devices):
            out[device, index] = block[device * piece : (device + 1) * piece, :]


def gram_blocks(place, factor, arrived, groups, devices):
    share, width = arrived[0].shape
    shape = (devices, groups * (groups - 1) // 2, width // devices, width)
    scratch = groups * share * width * 2 + groups * groups * width * width * 2
    return pl.pallas_call(
        functools.partial(gram_kernel, groups),
        out_shape=jax.ShapeDtypeStruct(shape, jnp.float32),
        in_specs=[SMEM, ANY] + [ANY] * (groups - 1),
        out_specs=VMEM,
        scratch_shapes=[
            pltpu.VMEM((groups, share, width), jnp.bfloat16),
            pltpu.VMEM((width, width), jnp.float32),
            pltpu.SemaphoreType.DMA((groups,)),
        ],
        compiler_params=pltpu.CompilerParams(vmem_limit_bytes=2 * scratch + 8 * 2**20),
        name="gram_blocks",
    )(place, factor, *arrived)


def assemble_kernel(devices, groups, place, *refs):
    pieces, outs = refs[:devices], refs[devices:]
    z, term = place[0], place[1]
    for k in range(devices):
        start = 0
        for out in outs:
            size = out.shape[1] // devices
            row = pl.multiple_of((term ^ k) * size, size)
            for r in range(groups):
                out[z ^ r, pl.ds(row, size), :] = pieces[k][r, start : start + size, :]
            start += size


def assemble(place, pieces, documents):
    groups, _, width = pieces[0].shape
    devices = len(pieces)
    return pl.pallas_call(
        functools.partial(assemble_kernel, devices, groups),
        out_shape=[
            jax.ShapeDtypeStruct((groups, rows, width), jnp.float32)
            for rows in (documents, documents, width)
        ],
        in_specs=[SMEM] + [VMEM] * devices,
        out_specs=[VMEM] * 3,
        compiler_params=pltpu.CompilerParams(
            vmem_limit_bytes=16 * groups * (2 * documents + width) * width + 4 * 2**20
        ),
        name="assemble",
    )(place, *pieces)


def dot3(left, right):
    dot = functools.partial(jnp.dot, preferred_element_type=jnp.float32)
    return dot(left[0], right[0]) + (dot(left[0], right[1]) + dot(left[1], right[0]))


def update_kernel(devices, groups, place, docs, codes, data, diagonal, stat, old, tiles, *rest):
    pieces = rest[:devices]
    codes_out, gram_new, data_new = rest[devices : devices + 3]
    high, low, cur, blocks, tile_buf, old_buf, piece_sem, tile_sem, old_sem, new_sem = rest[
        devices + 3 :
    ]
    z, term = place[0], place[1]
    width, documents = codes.shape[2], codes.shape[1]
    piece = width // devices
    landings = []
    for k in range(devices):
        row = pl.multiple_of((term ^ k) * piece, piece)
        copy = pltpu.make_async_copy(
            pieces[k], blocks.at[:, pl.ds(row, piece), :], piece_sem.at[k]
        )
        copy.start()
        landings.append(copy)
    rows = old.shape[0] // ROW_CHUNKS
    tile_in, old_in = [], []
    for chunk in range(ROW_CHUNKS):
        span = pl.ds(chunk * rows, rows)
        copy = pltpu.make_async_copy(tiles.at[span], tile_buf.at[span], tile_sem.at[chunk])
        copy.start()
        tile_in.append(copy)
        copy = pltpu.make_async_copy(old.at[span], old_buf.at[span], old_sem.at[chunk])
        copy.start()
        old_in.append(copy)
    for copy in landings:
        copy.wait()

    def place_block(i, j, value):
        at = (pl.ds(i * width, width), pl.ds(j * width, width))
        high[at], low[at] = split(value)

    for i in range(groups):
        place_block(i, i, diagonal[i])
        cur[:, pl.ds(i * width, width)] = codes[i]
    for index, (i, j) in enumerate(pairs_of(groups)):
        value = blocks[index]
        place_block(i, j, value)
        place_block(j, i, value.T)

    for _ in range(ITERS):
        applied = dot3(split(cur[...]), (high[...], low[...]))
        for i in range(groups):
            at = pl.ds(i * width, width)
            cur[:, at] = cur[:, at] * data[i] / (applied[:, i * width : (i + 1) * width] + EPSILON)

    own = cur[:, pl.ds(pl.multiple_of(z * width, width), width)]
    own_pair = split(own / documents)
    onehot = (
        lax.broadcasted_iota(jnp.int32, (documents, docs.shape[1]), 0) == docs[...]
    ).astype(jnp.bfloat16)
    picked = [contract_rows(onehot, value).astype(jnp.bfloat16) for value in own_pair]
    stacked = jnp.concatenate(picked, axis=0)
    stores = []
    for chunk in range(ROW_CHUNKS):
        span = pl.ds(chunk * rows, rows)
        tile_in[chunk].wait()
        old_in[chunk].wait()
        tile = tile_buf[span, :]
        old_buf[span, :] = DECAY * old_buf[span, :] + jnp.dot(
            jnp.concatenate([tile, tile], axis=1), stacked, preferred_element_type=jnp.float32
        )
        copy = pltpu.make_async_copy(old_buf.at[span], data_new.at[span], new_sem.at[chunk])
        copy.start()
        stores.append(copy)

    share = documents // devices
    codes_out[...] = cur[
        pl.ds(pl.multiple_of(term * share, share), share),
        pl.ds(pl.multiple_of(z * width, width), width),
    ]
    columns = stat.shape[0]
    first = term * columns
    group = first // width
    other = split(cur[:, pl.ds(pl.multiple_of(group * width, width), width)])
    blocks[0] = contract_rows(other[0], own_pair[0]) + (
        contract_rows(other[0], own_pair[1]) + contract_rows(other[1], own_pair[0])
    )
    offset = pl.multiple_of(first - group * width, columns)
    gram_new[...] = DECAY * stat[...] + blocks[0, pl.ds(offset, columns), :]
    for copy in stores:
        copy.wait()


def update(place, docs, codes, data, diagonal, stat, old, tiles, pieces):
    groups, documents, width = codes.shape
    topics = groups * width
    devices = len(pieces)
    return pl.pallas_call(
        functools.partial(update_kernel, devices, groups),
        out_shape=[
            jax.ShapeDtypeStruct((documents // devices, width), jnp.float32),
            jax.ShapeDtypeStruct(stat.shape, jnp.float32),
            jax.ShapeDtypeStruct(old.shape, jnp.float32),
        ],
        in_specs=[SMEM, VMEM, VMEM, VMEM, VMEM, VMEM, HBM, HBM] + [ANY] * devices,
        out_specs=[VMEM, VMEM, HBM],
        scratch_shapes=[
            pltpu.VMEM((topics, topics), jnp.bfloat16),
            pltpu.VMEM((topics, topics), jnp.bfloat16),
            pltpu.VMEM((documents, topics), jnp.float32),
            pltpu.VMEM((groups * (groups - 1) // 2, width, width), jnp.float32),
            pltpu.VMEM(tiles.shape, tiles.dtype),
            pltpu.VMEM(old.shape, old.dtype),
            pltpu.SemaphoreType.DMA((devices,)),
            pltpu.SemaphoreType.DMA((ROW_CHUNKS,)),
            pltpu.SemaphoreType.DMA((ROW_CHUNKS,)),
            pltpu.SemaphoreType.DMA((ROW_CHUNKS,)),
        ],
        compiler_params=pltpu.CompilerParams(
            vmem_limit_bytes=UPDATE_GRANT
        ),
        name="update",
    )(place, docs, codes, data, diagonal, stat, old, tiles, *pieces)


def exchange_order(groups):
    return [k for k in range(2, groups, 2)] + [k for k in range(1, groups, 2)]


def per_device(factor, tile_values, tile_docs, codes, gram_stat, data_stat):
    devices, groups = lax.axis_size("term"), lax.axis_size("topic")
    term, z = lax.axis_index("term"), lax.axis_index("topic")
    chips = devices // 2
    rows, width = factor.shape
    share = rows // groups
    mine = codes.shape[1]
    documents = mine * devices
    piece = width // devices
    place = jnp.stack([z, term]).astype(jnp.int32)

    order = exchange_order(groups)
    first, others = order[0], order[1:]

    def exchange(k, source):
        block = lax.dynamic_slice_in_dim(source, (z ^ k) * share, share, 0)
        return swap(block, "topic", k)

    arrived = {first: exchange(first, factor)}

    onehot = (
        jnp.arange(documents, dtype=jnp.int32)[:, None] == tile_docs[0][None, :]
    ).astype(jnp.float32)
    by_tile = contract_rows(tile_values, factor)
    data_part = jnp.dot(
        onehot, by_tile, precision=lax.Precision.HIGHEST, preferred_element_type=jnp.float32
    )
    diagonal_part = contract_rows(factor, factor)
    early = jnp.concatenate(
        [data_part.reshape(devices, mine, width), diagonal_part.reshape(devices, piece, width)],
        axis=1,
    )
    early = jnp.sum(lax.all_to_all(early, "term", 0, 0, tiled=True), axis=0)
    early = jnp.concatenate([codes.T, early], axis=0)
    by_group = [early] + [swap(early, "topic", k) for k in range(1, groups)]
    later, early = lax.optimization_barrier((factor, early))
    for k in others:
        arrived[k] = exchange(k, later)
    codes_all, data_all, diagonal_all = assemble(
        place, gather_term(jnp.stack(by_group), chips), documents
    )
    arrived, codes_all, data_all, diagonal_all = lax.optimization_barrier(
        (arrived, codes_all, data_all, diagonal_all)
    )
    blocks = gram_blocks(place, factor, [arrived[k] for k in range(1, groups)], groups, devices)
    total = jnp.sum(lax.all_to_all(blocks, "term", 0, 0, tiled=True), axis=0)
    whole = total
    for part in [swap(total, "topic", k) for k in order]:
        whole = whole + part
    pieces = gather_term(whole, chips)
    codes_out, gram_new, data_new = update(
        place, tile_docs, codes_all, data_all, diagonal_all, gram_stat.T, data_stat, tile_values, pieces
    )
    return codes_out.T, gram_new.T, data_new


def solution(mesh):
    placed = (
        P("term", "topic"),
        P("term", None),
        P("term", None),
        P("topic", "term"),
        P("topic", "term"),
        P("term", "topic"),
    )
    return jax.shard_map(
        per_device,
        mesh=mesh,
        in_specs=placed,
        out_specs=(P("topic", "term"), P("topic", "term"), P("term", "topic")),
        check_vma=False,
    )
```

```python
import functools
import jax
import jax.numpy as jnp
from jax import lax
from jax.experimental import pallas as pl
from jax.experimental.pallas import tpu as pltpu
from jax.sharding import PartitionSpec as P


ITERS = 3
EPSILON = 1e-06
DECAY = 0.5
ROW_CHUNKS = 4
UPDATE_GRANT = 48 * 2**20


VMEM = pl.BlockSpec(memory_space=pltpu.VMEM)
ANY = pl.BlockSpec(memory_space=pl.ANY)
HBM = pl.BlockSpec(memory_space=pltpu.HBM)
SMEM = pl.BlockSpec(memory_space=pltpu.SMEM)


def contract_rows(left, right):
    return lax.dot_general(
        left, right, (((0,), (0,)), ((), ())), preferred_element_type=jnp.float32
    )


def swap(value, axis, offset):
    return lax.ppermute(
        value, axis, [(i, i ^ offset) for i in range(lax.axis_size(axis))]
    )


def gather_term(piece, chips):
    near = [piece] + [swap(piece, "term", 2 * k) for k in range(1, chips)]
    far = [swap(value, "term", 1) for value in near]
    return [value for pair in zip(near, far) for value in pair]


def split(value):
    high = value.astype(jnp.bfloat16)
    return high, (value - high.astype(jnp.float32)).astype(jnp.bfloat16)


def pairs_of(count):
    return [(i, j) for i in range(count) for j in range(i + 1, count)]


def load_rows(offsets, place, factor, arrived, rows, sem):
    z = place[0]
    share = rows.shape[1]
    own = factor.at[pl.ds(pl.multiple_of(z * share, share), share)]
    copies = [pltpu.make_async_copy(own, rows.at[z], sem.at[0])]
    for index, (k, source) in enumerate(zip(offsets, arrived)):
        copies.append(pltpu.make_async_copy(source, rows.at[z ^ k], sem.at[index + 1]))
    for copy in copies:
        copy.start()
    for copy in copies:
        copy.wait()


def store_cut(out, index, block):
    devices, _, piece, _ = out.shape
    for device in range(devices):
        out[device, index] = block[device * piece : (device + 1) * piece, :]


def first_pairs_kernel(groups, offsets, place, factor, *rest):
    arrived = rest[: len(offsets)]
    out, rows, sem = rest[len(offsets) :]
    load_rows(offsets, place, factor, arrived, rows, sem)
    last = place[2]
    for index, (i, j) in enumerate(pairs_of(groups)):
        waits = jnp.logical_or(last == i, last == j)

        @pl.when(waits)
        def _():
            out[:, index] = jnp.zeros((out.shape[0],) + out.shape[2:], out.dtype)

        @pl.when(jnp.logical_not(waits))
        def _():
            store_cut(out, index, contract_rows(rows[i], rows[j]))


def last_pairs_kernel(groups, offsets, place, factor, *rest):
    arrived = rest[: len(offsets)]
    out, rows, sem = rest[len(offsets) :]
    load_rows(offsets, place, factor, arrived, rows, sem)
    last = place[2]
    for k in range(1, groups):
        other = last ^ k
        left, right = jnp.minimum(last, other), jnp.maximum(last, other)
        store_cut(out, k - 1, contract_rows(rows[left], rows[right]))


def pair_products(kernel, count, place, factor, offsets, arrived, groups, devices):
    share, width = arrived[0].shape
    shape = (devices, count, width // devices, width)
    grant = 4 * groups * share * width + 8 * devices * count * (width // devices) * width
    return pl.pallas_call(
        functools.partial(kernel, groups, offsets),
        out_shape=jax.ShapeDtypeStruct(shape, jnp.float32),
        in_specs=[SMEM, ANY] + [ANY] * len(offsets),
        out_specs=VMEM,
        scratch_shapes=[
            pltpu.VMEM((groups, share, width), jnp.bfloat16),
            pltpu.SemaphoreType.DMA((groups,)),
        ],
        compiler_params=pltpu.CompilerParams(vmem_limit_bytes=grant + 4 * 2**20),
    )(place, factor, *arrived)


def merge_kernel(groups, place, first, last, out):
    for index, (i, j) in enumerate(pairs_of(groups)):
        waits = jnp.logical_or(place[2] == i, place[2] == j)
        extra = last[0, (i ^ j) - 1]
        for device in range(1, last.shape[0]):
            extra = extra + last[device, (i ^ j) - 1]
        out[index] = first[index] + jnp.where(waits, extra, 0.0)


def merge(place, first, last, groups):
    return pl.pallas_call(
        functools.partial(merge_kernel, groups),
        out_shape=jax.ShapeDtypeStruct(first.shape, jnp.float32),
        in_specs=[SMEM, VMEM, VMEM],
        out_specs=VMEM,
        compiler_params=pltpu.CompilerParams(
            vmem_limit_bytes=8 * (2 * first.size + last.size) + 2 * 2**20
        ),
        name="merge",
    )(place, first, last)


def assemble_kernel(devices, groups, place, *refs):
    pieces, outs = refs[:devices], refs[devices:]
    z, term = place[0], place[1]
    for k in range(devices):
        start = 0
        for out in outs:
            size = out.shape[1] // devices
            row = pl.multiple_of((term ^ k) * size, size)
            for r in range(groups):
                out[z ^ r, pl.ds(row, size), :] = pieces[k][r, start : start + size, :]
            start += size


def assemble(place, pieces, documents):
    groups, _, width = pieces[0].shape
    devices = len(pieces)
    return pl.pallas_call(
        functools.partial(assemble_kernel, devices, groups),
        out_shape=[
            jax.ShapeDtypeStruct((groups, rows, width), jnp.float32)
            for rows in (documents, documents, width)
        ],
        in_specs=[SMEM] + [VMEM] * devices,
        out_specs=[VMEM] * 3,
        compiler_params=pltpu.CompilerParams(
            vmem_limit_bytes=16 * groups * (2 * documents + width) * width + 4 * 2**20
        ),
        name="assemble",
    )(place, *pieces)


def dot3(left, right):
    dot = functools.partial(jnp.dot, preferred_element_type=jnp.float32)
    return dot(left[0], right[0]) + (dot(left[0], right[1]) + dot(left[1], right[0]))


def update_kernel(devices, groups, place, docs, codes, data, diagonal, stat, old, tiles, *rest):
    pieces = rest[:devices]
    codes_out, gram_new, data_new = rest[devices : devices + 3]
    high, low, cur, blocks, new, piece_sem, old_sem, new_sem = rest[devices + 3 :]
    z, term = place[0], place[1]
    width, documents = codes.shape[2], codes.shape[1]
    piece = width // devices
    landings = []
    for k in range(devices):
        row = pl.multiple_of((term ^ k) * piece, piece)
        copy = pltpu.make_async_copy(
            pieces[k], blocks.at[:, pl.ds(row, piece), :], piece_sem.at[k]
        )
        copy.start()
        landings.append(copy)
    rows = old.shape[0] // ROW_CHUNKS
    spans = [pl.ds(chunk * rows, rows) for chunk in range(ROW_CHUNKS)]
    loads = [
        pltpu.make_async_copy(old.at[span], new.at[span], old_sem.at[chunk])
        for chunk, span in enumerate(spans)
    ]
    for copy in loads:
        copy.start()
    for copy in landings:
        copy.wait()

    def place_block(i, j, value):
        at = (pl.ds(i * width, width), pl.ds(j * width, width))
        high[at], low[at] = split(value)

    for i in range(groups):
        place_block(i, i, diagonal[i])
        cur[:, pl.ds(i * width, width)] = codes[i]
    for index, (i, j) in enumerate(pairs_of(groups)):
        value = blocks[index]
        place_block(i, j, value)
        place_block(j, i, value.T)

    for _ in range(ITERS):
        applied = dot3(split(cur[...]), (high[...], low[...]))
        for i in range(groups):
            at = pl.ds(i * width, width)
            cur[:, at] = cur[:, at] * data[i] / (applied[:, i * width : (i + 1) * width] + EPSILON)

    own = cur[:, pl.ds(pl.multiple_of(z * width, width), width)]
    own_pair = split(own / documents)
    onehot = (
        lax.broadcasted_iota(jnp.int32, (documents, docs.shape[1]), 0) == docs[...]
    ).astype(jnp.bfloat16)
    picked = [contract_rows(onehot, value).astype(jnp.bfloat16) for value in own_pair]
    stacked = jnp.concatenate(picked, axis=0)
    stores = []
    for chunk, span in enumerate(spans):
        tile = tiles[span, :]
        loads[chunk].wait()
        new[span, :] = DECAY * new[span, :] + jnp.dot(
            jnp.concatenate([tile, tile], axis=1), stacked, preferred_element_type=jnp.float32
        )
        copy = pltpu.make_async_copy(new.at[span], data_new.at[span], new_sem.at[chunk])
        copy.start()
        stores.append(copy)

    share = documents // devices
    codes_out[...] = cur[
        pl.ds(pl.multiple_of(term * share, share), share),
        pl.ds(pl.multiple_of(z * width, width), width),
    ]
    columns = stat.shape[0]
    first = term * columns
    group = first // width
    other = split(cur[:, pl.ds(pl.multiple_of(group * width, width), width)])
    blocks[0] = contract_rows(other[0], own_pair[0]) + (
        contract_rows(other[0], own_pair[1]) + contract_rows(other[1], own_pair[0])
    )
    offset = pl.multiple_of(first - group * width, columns)
    gram_new[...] = DECAY * stat[...] + blocks[0, pl.ds(offset, columns), :]
    for copy in stores:
        copy.wait()


def update(place, docs, codes, data, diagonal, stat, old, tiles, pieces):
    groups, documents, width = codes.shape
    topics = groups * width
    devices = len(pieces)
    return pl.pallas_call(
        functools.partial(update_kernel, devices, groups),
        out_shape=[
            jax.ShapeDtypeStruct((documents // devices, width), jnp.float32),
            jax.ShapeDtypeStruct(stat.shape, jnp.float32),
            jax.ShapeDtypeStruct(old.shape, jnp.float32),
        ],
        in_specs=[SMEM, VMEM, VMEM, VMEM, VMEM, VMEM, HBM, VMEM] + [ANY] * devices,
        out_specs=[VMEM, VMEM, HBM],
        scratch_shapes=[
            pltpu.VMEM((topics, topics), jnp.bfloat16),
            pltpu.VMEM((topics, topics), jnp.bfloat16),
            pltpu.VMEM((documents, topics), jnp.float32),
            pltpu.VMEM((groups * (groups - 1) // 2, width, width), jnp.float32),
            pltpu.VMEM(old.shape, old.dtype),
            pltpu.SemaphoreType.DMA((devices,)),
            pltpu.SemaphoreType.DMA((ROW_CHUNKS,)),
            pltpu.SemaphoreType.DMA((ROW_CHUNKS,)),
        ],
        compiler_params=pltpu.CompilerParams(
            vmem_limit_bytes=UPDATE_GRANT
        ),
        name="update",
    )(
        place, docs, codes, data, diagonal, stat,
        old, tiles,
        *pieces,
    )


def exchange_order(groups):
    return [k for k in range(2, groups, 2)] + [k for k in range(1, groups, 2)]


def per_device(factor, tile_values, tile_docs, codes, gram_stat, data_stat):
    devices, groups = lax.axis_size("term"), lax.axis_size("topic")
    term, z = lax.axis_index("term"), lax.axis_index("topic")
    chips = devices // 2
    rows, width = factor.shape
    share = rows // groups
    mine = codes.shape[1]
    documents = mine * devices
    piece = width // devices
    order = exchange_order(groups)
    place = jnp.stack([z, term, z ^ order[-1]]).astype(jnp.int32)

    def exchange(k, source):
        block = lax.dynamic_slice_in_dim(source, (z ^ k) * share, share, 0)
        return swap(block, "topic", k)

    arrived = {k: exchange(k, factor) for k in order[:-1]}

    onehot = (
        jnp.arange(documents, dtype=jnp.int32)[:, None] == tile_docs[0][None, :]
    ).astype(jnp.float32)
    by_tile = contract_rows(tile_values, factor)
    data_part = jnp.dot(
        onehot, by_tile, precision=lax.Precision.HIGHEST, preferred_element_type=jnp.float32
    )
    diagonal_part = contract_rows(factor, factor)
    early = jnp.concatenate(
        [data_part.reshape(devices, mine, width), diagonal_part.reshape(devices, piece, width)],
        axis=1,
    )
    early = jnp.sum(lax.all_to_all(early, "term", 0, 0, tiled=True), axis=0)
    early = jnp.concatenate([codes.T, early], axis=0)
    by_group = [early] + [swap(early, "topic", k) for k in range(1, groups)]
    later, early = lax.optimization_barrier((factor, early))
    arrived[order[-1]] = exchange(order[-1], later)
    codes_all, data_all, diagonal_all = assemble(
        place, gather_term(jnp.stack(by_group), chips), documents
    )
    blocks = pair_products(
        first_pairs_kernel, groups * (groups - 1) // 2,
        place, factor, order[:-1], [arrived[k] for k in order[:-1]], groups, devices,
    )
    first = jnp.sum(lax.all_to_all(blocks, "term", 0, 0, tiled=True), axis=0)
    arrived, codes_all, data_all, diagonal_all, first = lax.optimization_barrier(
        (arrived, codes_all, data_all, diagonal_all, first)
    )

    blocks = pair_products(
        last_pairs_kernel, groups - 1,
        place, factor, order, [arrived[k] for k in order], groups, devices,
    )
    total = merge(place, first, lax.all_to_all(blocks, "term", 0, 0, tiled=True), groups)
    whole = total
    for part in [swap(total, "topic", k) for k in order]:
        whole = whole + part
    pieces = gather_term(whole, chips)
    codes_out, gram_new, data_new = update(
        place, tile_docs, codes_all, data_all, diagonal_all, gram_stat.T, data_stat, tile_values, pieces
    )
    return codes_out.T, gram_new.T, data_new


def solution(mesh):
    placed = (
        P("term", "topic"),
        P("term", None),
        P("term", None),
        P("topic", "term"),
        P("topic", "term"),
        P("term", "topic"),
    )
    return jax.shard_map(
        per_device,
        mesh=mesh,
        in_specs=placed,
        out_specs=(P("topic", "term"), P("topic", "term"), P("term", "topic")),
        check_vma=False,
    )
```
